32 devices in a mesh: grp: 2 (over core), dev: 16 (over z, y, x).
Axes of the slice: x: 2, y: 2, z: 4, core: 2. Of those that a mesh axis runs over, the one named last changes fastest.
Arguments:
- queries: float32 [32, 12, 128], P(('grp', 'dev')), may hold values from -2.1 to 2.1
- pages: float32 [32, 256, 128], P(('grp', 'dev')), may hold values from -2.1 to 2.1
- positive: int32 [32], replicated, may hold values from 0 to 31
Outputs:
- loss: float32 [], replicated
- question_token_slope: float32 [32, 12, 128], P(('grp', 'dev'))
- page_grad: float32 [32, 256, 128], P(('grp', 'dev'))
The draws below stay inside these ranges and needn't reach their ends.
All inputs are finite; a program needn't handle non-finite values.
Results may differ from the reference program's by a relative error of at most 0.00019.
Values sent between devices are 32-bit elements; how exact they have to be, the bound alone decides.
A program may use at most 64 MiB of HBM per device.

```python
import jax
import jax.numpy as jnp
from jax import lax

W = 128
QTOK = 12
PAGE_TOK = 256
NQ = 32
NP = 32


def with_ends(result, own_key, least, largest):
    place = [jax.random.randint(jax.random.fold_in(own_key, axis), (), 0, length) for axis, length in enumerate(result.shape)]
    main_axis = result.shape.index(max(result.shape))
    neighbour = place[:main_axis] + [(place[main_axis] + 1) % result.shape[main_axis]] + place[main_axis + 1:]
    return result.at[tuple(place)].set(least).at[tuple(neighbour)].set(largest)


def steps_of(key, dims, cuts, least, largest):
    loudness = 1.0
    for dim, shards_of in cuts:
        draws = jax.random.uniform(jax.random.fold_in(jax.random.fold_in(key, 6), dim), (shards_of,), jnp.float32, least / len(cuts), largest / len(cuts))
        loudness = loudness * jnp.repeat(jnp.exp(draws), dims[dim] // shards_of).reshape((-1,) + (1,) * (len(dims) - 1 - dim))
    return loudness


def scatter_about(rng, extent, width, most, shards=(), held_as=jnp.bfloat16):
    values = jax.random.normal(rng, extent, jnp.float32) * width
    if len(shards) > 0:
        values = steps_of(rng, extent, shards, -0.22, 0.18) * values
    return jnp.clip(values, min=-most, max=most).astype(held_as)


def setup_inputs(seed: int = 0) -> dict:
    splits = jax.random.split(jax.random.key(seed), 4)
    queries = scatter_about(splits[0], (NQ, QTOK, W), 0.35, 2.1, ((0, 32),), jnp.float32)
    pages = scatter_about(splits[1], (NP, PAGE_TOK, W), 0.35, 2.1, ((0, 32),), jnp.float32)
    positive = with_ends(jax.random.randint(splits[2], (NQ,), 0, NP), jax.random.fold_in(splits[2], 1), 0, NP - 1).astype(jnp.int32)
    return dict(queries=queries, pages=pages, positive=positive)


cap_value = 4.0
sharpness_divisor = 0.25
logit_scale = 8.0
z_weight = 0.001
highest = lax.Precision.HIGHEST


def block_partial_terms(query_rows, page_rows, query_tokens):
    scores = jnp.dot(query_rows, page_rows.T, precision=highest, preferred_element_type=jnp.float32)
    tangent = jnp.tanh(scores / cap_value)
    bounded_similarity = cap_value * tangent
    exponential_grid = jnp.exp(bounded_similarity / sharpness_divisor)
    accumulated_totals = jnp.sum(exponential_grid, axis=1)
    gentle_peak = sharpness_divisor * jnp.log(accumulated_totals)
    slopes = exponential_grid / accumulated_totals[:, None] * (1.0 - tangent * tangent) * (logit_scale / query_tokens)
    return gentle_peak, slopes


def reference(queries, pages, positive):
    flattened_query_rows = queries.reshape(NQ * QTOK, W)

    def page_logits(page_rows):
        gentle_peak, unused_slopes = block_partial_terms(flattened_query_rows, page_rows, QTOK)
        return logit_scale / QTOK * gentle_peak.reshape(NQ, QTOK).sum(axis=1)

    logits = lax.map(page_logits, pages)
    exponential_grid = jnp.exp(logits)
    accumulated_totals = jnp.sum(exponential_grid, axis=0)
    log_totals = jnp.log(accumulated_totals)
    chosen = (positive[None, :] == jnp.arange(NP, dtype=jnp.int32)[:, None]).astype(jnp.float32)
    matching_logit = jnp.sum(chosen * logits, axis=0)
    loss = jnp.mean(log_totals - matching_logit + z_weight * log_totals * log_totals)
    coefficients = ((1.0 + 2.0 * z_weight * log_totals)[None, :] * exponential_grid / accumulated_totals[None, :] - chosen) / NQ

    def backward(query_total, inputs):
        page_rows, column = inputs
        unused_smooth, slopes = block_partial_terms(flattened_query_rows, page_rows, QTOK)
        token_grads = slopes * jnp.repeat(column, QTOK)[:, None]
        query_total = query_total + jnp.dot(token_grads, page_rows, precision=highest, preferred_element_type=jnp.float32)
        page_part = jnp.dot(token_grads.T, flattened_query_rows, precision=highest, preferred_element_type=jnp.float32)
        return query_total, page_part

    start_total = jnp.zeros((NQ * QTOK, W), jnp.float32)
    query_total, page_grad = lax.scan(backward, start_total, (pages, coefficients))
    return loss, query_total.reshape(NQ, QTOK, W), page_grad
```

```python
import functools
import math

import jax
import jax.numpy as jnp
from jax import lax
from jax.experimental import pallas as pl
from jax.experimental.pallas import tpu as pltpu
from jax.sharding import PartitionSpec as P

cap_value = 4.0
sharpness_divisor = 0.25
logit_scale = 8.0
z_weight = 0.001
highest = lax.Precision.HIGHEST
MESH = pl.DeviceIdType.MESH


def split(x):
    high = x.astype(jnp.bfloat16)
    low = (x - high.astype(jnp.float32)).astype(jnp.bfloat16)
    return high, low


def dot(a, b):
    return jnp.dot(a, b, preferred_element_type=jnp.float32)


def dot3(a, b):
    (a_high, a_low), (b_high, b_low) = a, b
    return dot(a_high, b_high) + (dot(a_high, b_low) + dot(a_low, b_high))


def kernel(
    groups, members, block, pad,
    query_hbm, page_hbm, positive_hbm,
    loss_ref, query_grad_hbm, page_grad_hbm,
    gathered, page, positive, rows, slopes_of, slopes_t, own_logits, logits, terms, arrived,
    weights, page_grad, query_grad,
    query_sem, page_sem, positive_sem, out_sems, send_sems, recv_sems,
):
    count = groups * members
    blocks = count // block
    tokens = gathered.shape[1]
    lanes = own_logits.shape[-1]
    block_rows = block * pad
    group, member = lax.axis_index("grp"), lax.axis_index("dev")
    me = group * members + member

    def place(k):
        peer = lax.rem(me + k, count)
        return peer, (peer // members, lax.rem(peer, members))

    query_copy = pltpu.make_async_copy(query_hbm.at[0], gathered.at[me], query_sem)
    page_copy = pltpu.make_async_copy(page_hbm.at[0], page, page_sem)
    positive_copy = pltpu.make_async_copy(positive_hbm, positive, positive_sem)
    query_copy.start()
    page_copy.start()
    positive_copy.start()

    barrier = pltpu.get_barrier_semaphore()

    def greet(k, carry):
        _, device = place(k)
        pl.semaphore_signal(barrier, inc=1, device_id=device, device_id_type=MESH)
        return carry

    lax.fori_loop(1, count, greet, 0)
    query_copy.wait()
    pl.semaphore_wait(barrier, count - 1)

    def send_query(k, carry):
        _, device = place(k)
        pltpu.make_async_remote_copy(
            gathered.at[me], gathered.at[me], send_sems.at[0], recv_sems.at[0],
            device_id=device, device_id_type=MESH,
        ).start()
        return carry

    lax.fori_loop(1, count, send_query, 0)

    def wait_all(buffer, sem):
        whole = buffer.at[pl.ds(0, count - 1)]
        pltpu.make_async_copy(whole, whole, sem).wait()

    page_copy.wait()
    positive_copy.wait()
    page_rows = page[...]
    page_columns = page_rows.T
    page_parts = split(page_rows)
    rows[...] = jnp.zeros_like(rows)
    wait_all(gathered, recv_sems.at[0])

    def score(b, logit_row):
        for q in range(block):
            rows[b, q * pad:q * pad + tokens, :] = gathered[b * block + q]
        scores = jnp.dot(
            rows[b], page_columns, precision=highest, preferred_element_type=jnp.float32
        )
        tangent = jnp.tanh(scores / cap_value)
        grid = jnp.exp(tangent * (cap_value / sharpness_divisor))
        totals = jnp.sum(grid, axis=1, keepdims=True)
        peak = sharpness_divisor * jnp.log(totals)
        slopes = grid * (1.0 - tangent * tangent) * ((logit_scale / tokens) / totals)
        slopes_of[b] = slopes
        row = lax.broadcasted_iota(jnp.int32, (block_rows, lanes), 0)
        lane = lax.broadcasted_iota(jnp.int32, (block_rows, lanes), 1)
        mine = (lane == b * block + row // pad) & (row % pad < tokens)
        return logit_row + jnp.sum(jnp.where(mine, peak, 0.0), axis=0, keepdims=True)

    logit_row = lax.fori_loop(0, blocks, score, jnp.zeros((1, lanes), jnp.float32))
    own_logits[...] = logit_row * (logit_scale / tokens)
    logits[me] = own_logits[...]

    def send_logits(k, carry):
        _, device = place(k)
        pltpu.make_async_remote_copy(
            own_logits, logits.at[me], send_sems.at[1], recv_sems.at[1],
            device_id=device, device_id_type=MESH,
        ).start()
        return carry

    lax.fori_loop(1, count, send_logits, 0)

    def project(b, carry):
        slopes = slopes_of[b]
        term = dot3(split(slopes), page_parts)
        for q in range(block):
            terms[b * block + q] = term[q * pad:q * pad + tokens, :]
        slopes_t[b] = slopes.T
        return carry

    lax.fori_loop(0, blocks, project, 0)

    def send_terms(k, carry):
        peer, device = place(k)
        pltpu.make_async_remote_copy(
            terms.at[peer], arrived.at[me], send_sems.at[2], recv_sems.at[2],
            device_id=device, device_id_type=MESH,
        ).start()
        return carry

    lax.fori_loop(1, count, send_terms, 0)

    wait_all(logits, recv_sems.at[1])
    table = logits[:, 0, :][:, :count]
    of_page = lax.broadcasted_iota(jnp.int32, (count, count), 0)
    of_query = lax.broadcasted_iota(jnp.int32, (count, count), 1)
    chosen = (positive[...] == of_page).astype(jnp.float32)
    grid = jnp.exp(table)
    totals = jnp.sum(grid, axis=0, keepdims=True)
    log_totals = jnp.log(totals)
    matching = jnp.sum(chosen * table, axis=0, keepdims=True)
    losses = log_totals - matching + z_weight * log_totals * log_totals
    loss_ref[...] = jnp.sum(losses, axis=1, keepdims=True) / count
    coefficients = ((1.0 + 2.0 * z_weight * log_totals) * grid / totals - chosen) / count
    of_me = jnp.sum(jnp.where(of_page == me, coefficients, 0.0), axis=0, keepdims=True)
    to_me = jnp.sum(jnp.where(of_query == me, coefficients, 0.0), axis=1, keepdims=True)
    weights[...] = jnp.broadcast_to(to_me, weights.shape)

    def gather_page(b, total):
        row = lax.broadcasted_iota(jnp.int32, (block_rows, count), 0)
        lane = lax.broadcasted_iota(jnp.int32, (block_rows, count), 1)
        mine = lane == b * block + row // pad
        factor = jnp.sum(jnp.where(mine, of_me, 0.0), axis=1, keepdims=True)
        return total + dot3(split(slopes_t[b]), split(rows[b] * factor))

    page_grad[...] = lax.fori_loop(0, blocks, gather_page, jnp.zeros(page_grad.shape, jnp.float32))
    page_out = pltpu.make_async_copy(page_grad, page_grad_hbm.at[0], out_sems.at[0])
    page_out.start()

    wait_all(arrived, recv_sems.at[2])
    arrived[me] = terms[me]

    def gather_query(p, total):
        return total + arrived[p] * weights[pl.ds(p, 1), :]

    query_grad[...] = lax.fori_loop(
        0, count, gather_query, jnp.zeros(query_grad.shape, jnp.float32), unroll=8
    )
    query_out = pltpu.make_async_copy(query_grad, query_grad_hbm.at[0], out_sems.at[1])
    query_out.start()
    wait_all(gathered, send_sems.at[0])
    wait_all(logits, send_sems.at[1])
    wait_all(terms, send_sems.at[2])
    page_out.wait()
    query_out.wait()


def shards(groups, members, queries, pages, positive):
    count = groups * members
    _, tokens, width = queries.shape
    page_tokens = pages.shape[1]
    block = math.gcd(count, 16)
    blocks = count // block
    pad = -(-tokens // 8) * 8
    lanes = max(128, -(-count // 128) * 128)
    anywhere = pl.BlockSpec(memory_space=pl.ANY)
    float32 = jnp.float32
    loss, query_grad, page_grad = pl.pallas_call(
        functools.partial(kernel, groups, members, block, pad),
        out_shape=(
            jax.ShapeDtypeStruct((1, 1), float32),
            jax.ShapeDtypeStruct(queries.shape, float32),
            jax.ShapeDtypeStruct(pages.shape, float32),
        ),
        in_specs=[anywhere] * 3,
        out_specs=(pl.BlockSpec(memory_space=pltpu.VMEM), anywhere, anywhere),
        scratch_shapes=[
            pltpu.VMEM((count, tokens, width), float32),
            pltpu.VMEM((page_tokens, width), float32),
            pltpu.VMEM((1, count), jnp.int32),
            pltpu.VMEM((blocks, block * pad, width), float32),
            pltpu.VMEM((blocks, block * pad, page_tokens), float32),
            pltpu.VMEM((blocks, page_tokens, block * pad), float32),
            pltpu.VMEM((1, lanes), float32),
            pltpu.VMEM((count, 1, lanes), float32),
            pltpu.VMEM((count, tokens, width), float32),
            pltpu.VMEM((count, tokens, width), float32),
            pltpu.VMEM((count, width), float32),
            pltpu.VMEM((page_tokens, width), float32),
            pltpu.VMEM((tokens, width), float32),
            pltpu.SemaphoreType.DMA,
            pltpu.SemaphoreType.DMA,
            pltpu.SemaphoreType.DMA,
            pltpu.SemaphoreType.DMA((2,)),
            pltpu.SemaphoreType.DMA((3,)),
            pltpu.SemaphoreType.DMA((3,)),
        ],
        compiler_params=pltpu.CompilerParams(collective_id=0, has_side_effects=True),
    )(queries, pages, positive.reshape(1, count))
    return loss.reshape(()), query_grad, page_grad


def solution(mesh):
    groups, members = mesh.shape["grp"], mesh.shape["dev"]
    split_spec = P(("grp", "dev"), None, None)
    return jax.shard_map(
        functools.partial(shards, groups, members),
        mesh=mesh,
        in_specs=(split_spec, split_spec, P()),
        out_specs=(P(), split_spec, split_spec),
        check_vma=False,
    )
```

```python
import functools
import math

import jax
import jax.numpy as jnp
from jax import lax
from jax.experimental import pallas as pl
from jax.experimental.pallas import tpu as pltpu
from jax.sharding import PartitionSpec as P

cap_value = 4.0
sharpness_divisor = 0.25
logit_scale = 8.0
z_weight = 0.001
highest = lax.Precision.HIGHEST
MESH = pl.DeviceIdType.MESH


def split(x):
    high = x.astype(jnp.bfloat16)
    low = (x - high.astype(jnp.float32)).astype(jnp.bfloat16)
    return high, low


def dot(a, b):
    return jnp.dot(a, b, preferred_element_type=jnp.float32)


def dot3(a, b):
    (a_high, a_low), (b_high, b_low) = a, b
    return dot(a_high, b_high) + (dot(a_high, b_low) + dot(a_low, b_high))


def kernel(
    groups, members, block, pad,
    query_hbm, page_hbm, positive_hbm,
    query_grad, page_grad,
    gathered, page, positive, rows, slopes_t, own_logits, logits, terms, arrived, weights,
    query_sem, page_sem, positive_sem, send_sems, recv_sems,
):
    count = groups * members
    group_blocks = members // block
    blocks = groups * group_blocks
    tokens = gathered.shape[1]
    lanes = own_logits.shape[-1]
    block_rows = block * pad
    group, member = lax.axis_index("grp"), lax.axis_index("dev")
    me = group * members + member

    query_copy = pltpu.make_async_copy(query_hbm.at[:, 0], gathered.at[me], query_sem)
    page_copy = pltpu.make_async_copy(page_hbm.at[0], page, page_sem)
    positive_copy = pltpu.make_async_copy(positive_hbm, positive, positive_sem)
    query_copy.start()
    page_copy.start()
    positive_copy.start()

    def each(first, last, act):
        def step(k, carry):
            to_group = lax.rem(group + k // members, groups)
            to_member = lax.rem(member + k, members)
            act(to_group * members + to_member, (to_group, to_member))
            return carry

        lax.fori_loop(first, last, step, 0)

    def send(source, target, stage, device):
        pltpu.make_async_remote_copy(
            source, target, send_sems.at[stage], recv_sems.at[stage],
            device_id=device, device_id_type=MESH,
        ).start()

    def wait_all(buffer, size, sem):
        whole = buffer.at[pl.ds(0, size)]
        pltpu.make_async_copy(whole, whole, sem).wait()

    barrier = pltpu.get_barrier_semaphore()
    each(1, count, lambda peer, device: pl.semaphore_signal(
        barrier, inc=1, device_id=device, device_id_type=MESH))
    query_copy.wait()
    pl.semaphore_wait(barrier, count - 1)
    each(1, members, lambda peer, device: send(gathered.at[me], gathered.at[me], 0, device))

    page_copy.wait()
    positive_copy.wait()
    page_rows = page[...]
    page_columns = page_rows.T
    page_parts = split(page_rows)
    rows[...] = jnp.zeros_like(rows)

    def score(b, logit_row):
        for q in range(block):
            rows[b, q * pad:q * pad + tokens, :] = gathered[b * block + q]
        scores = jnp.dot(
            rows[b], page_columns, precision=highest, preferred_element_type=jnp.float32
        )
        tangent = jnp.tanh(scores / cap_value)
        grid = jnp.exp(tangent * (cap_value / sharpness_divisor))
        totals = jnp.sum(grid, axis=1, keepdims=True)
        peak = sharpness_divisor * jnp.log(totals)
        slopes = grid * (1.0 - tangent * tangent) * ((logit_scale / tokens) / totals)
        term = dot3(split(slopes), page_parts)
        for q in range(block):
            terms[b * block + q] = term[q * pad:q * pad + tokens, :]
        slopes_t[b] = slopes.T
        row = lax.broadcasted_iota(jnp.int32, (block_rows, lanes), 0)
        lane = lax.broadcasted_iota(jnp.int32, (block_rows, lanes), 1)
        mine = (lane == b * block + row // pad) & (row % pad < tokens)
        return logit_row + jnp.sum(jnp.where(mine, peak, 0.0), axis=0, keepdims=True)

    def score_from(s, logit_row):
        return score(lax.rem(group * group_blocks + s, blocks), logit_row)

    def send_term(peer, device):
        send(terms.at[peer], arrived.at[me], 3, device)

    wait_all(gathered, members - 1, recv_sems.at[0])
    own_group = gathered.at[pl.ds(group * members, members)]

    def pass_on(k, carry):
        send(own_group, own_group, 1, (lax.rem(group + k, groups), member))
        return carry

    lax.fori_loop(1, groups, pass_on, 0)
    logit_row = jnp.zeros((1, lanes), jnp.float32)
    logit_row = lax.fori_loop(0, group_blocks, score_from, logit_row)
    each(1, members, send_term)
    wait_all(gathered, count - members, recv_sems.at[1])
    logit_row = lax.fori_loop(group_blocks, blocks, score_from, logit_row)
    own_logits[...] = logit_row * (logit_scale / tokens)
    logits[me] = own_logits[...]
    each(1, count, lambda peer, device: send(own_logits, logits.at[me], 2, device))
    each(members, count, send_term)

    wait_all(logits, count - 1, recv_sems.at[2])
    table = logits[:, 0, :][:, :count]
    of_page = lax.broadcasted_iota(jnp.int32, (count, count), 0)
    of_query = lax.broadcasted_iota(jnp.int32, (count, count), 1)
    chosen = (positive[...] == of_page).astype(jnp.float32)
    grid = jnp.exp(table)
    totals = jnp.sum(grid, axis=0, keepdims=True)
    log_totals = jnp.log(totals)
    matching = jnp.sum(chosen * table, axis=0, keepdims=True)
    losses = log_totals - matching + z_weight * log_totals * log_totals
    loss = jnp.sum(losses, axis=1, keepdims=True) / count
    query_grad[tokens] = jnp.broadcast_to(loss, query_grad.shape[1:])
    coefficients = ((1.0 + 2.0 * z_weight * log_totals) * grid / totals - chosen) / count
    of_me = jnp.sum(jnp.where(of_page == me, coefficients, 0.0), axis=0, keepdims=True)
    to_me = jnp.sum(jnp.where(of_query == me, coefficients, 0.0), axis=1, keepdims=True)
    weights[...] = jnp.broadcast_to(to_me, weights.shape)

    def gather_page(b, total):
        row = lax.broadcasted_iota(jnp.int32, (block_rows, count), 0)
        lane = lax.broadcasted_iota(jnp.int32, (block_rows, count), 1)
        mine = lane == b * block + row // pad
        factor = jnp.sum(jnp.where(mine, of_me, 0.0), axis=1, keepdims=True)
        return total + dot3(split(slopes_t[b]), split(rows[b] * factor))

    page_grad[...] = lax.fori_loop(0, blocks, gather_page, jnp.zeros(page_grad.shape, jnp.float32))

    wait_all(arrived, count - 1, recv_sems.at[3])
    arrived[me] = terms[me]

    def gather_query(p, total):
        return total + arrived[p] * weights[pl.ds(p, 1), :]

    total = lax.fori_loop(
        0, count, gather_query, jnp.zeros(arrived.shape[1:], jnp.float32), unroll=8
    )
    for i in range(tokens):
        query_grad[i] = total[i:i + 1, :]
    wait_all(gathered, members - 1, send_sems.at[0])
    wait_all(gathered, count - members, send_sems.at[1])
    wait_all(logits, count - 1, send_sems.at[2])
    wait_all(terms, count - 1, send_sems.at[3])


def hand_over(query_grad, page_grad, loss_hbm, query_grad_hbm, page_grad_hbm, loss, sems):
    tokens = query_grad_hbm.shape[0]
    page_out = pltpu.make_async_copy(page_grad, page_grad_hbm.at[0], sems.at[0])
    query_out = pltpu.make_async_copy(
        query_grad.at[pl.ds(0, tokens)], query_grad_hbm, sems.at[1]
    )
    loss_out = pltpu.make_async_copy(loss, loss_hbm, sems.at[2])
    page_out.start()
    query_out.start()
    loss[...] = query_grad[tokens][:, :1]
    loss_out.start()
    page_out.wait()
    query_out.wait()
    loss_out.wait()


def shards(groups, members, queries, pages, positive):
    count = groups * members
    _, tokens, width = queries.shape
    page_tokens = pages.shape[1]
    block = math.gcd(members, 16)
    blocks = count // block
    pad = -(-tokens // 8) * 8
    lanes = max(128, -(-count // 128) * 128)
    anywhere = pl.BlockSpec(memory_space=pl.ANY)
    vmem = pl.BlockSpec(memory_space=pltpu.VMEM)
    float32 = jnp.float32
    results = pl.pallas_call(
        functools.partial(kernel, groups, members, block, pad),
        out_shape=(
            pltpu.VMEM((tokens + 1, 1, width), float32),
            pltpu.VMEM((page_tokens, width), float32),
        ),
        in_specs=[anywhere] * 3,
        out_specs=(vmem,) * 2,
        scratch_shapes=[
            pltpu.VMEM((count, tokens, width), float32),
            pltpu.VMEM((page_tokens, width), float32),
            pltpu.VMEM((1, count), jnp.int32),
            pltpu.VMEM((blocks, block * pad, width), float32),
            pltpu.VMEM((blocks, page_tokens, block * pad), float32),
            pltpu.VMEM((1, lanes), float32),
            pltpu.VMEM((count, 1, lanes), float32),
            pltpu.VMEM((count, tokens, width), float32),
            pltpu.VMEM((count, tokens, width), float32),
            pltpu.VMEM((count, width), float32),
            pltpu.SemaphoreType.DMA,
            pltpu.SemaphoreType.DMA,
            pltpu.SemaphoreType.DMA,
            pltpu.SemaphoreType.DMA((4,)),
            pltpu.SemaphoreType.DMA((4,)),
        ],
        compiler_params=pltpu.CompilerParams(collective_id=0, has_side_effects=True),
    )(jnp.transpose(queries, (1, 0, 2)), pages, positive.reshape(1, count))
    loss, query_grad, page_grad = pl.pallas_call(
        hand_over,
        out_shape=(
            jax.ShapeDtypeStruct((1, 1), float32),
            jax.ShapeDtypeStruct((tokens, 1, width), float32),
            jax.ShapeDtypeStruct(pages.shape, float32),
        ),
        in_specs=[vmem] * 2,
        out_specs=(anywhere,) * 3,
        scratch_shapes=[pltpu.VMEM((1, 1), float32), pltpu.SemaphoreType.DMA((3,))],
        compiler_params=pltpu.CompilerParams(vmem_limit_bytes=1 << 20),
    )(*[pltpu.with_memory_space_constraint(x, pltpu.VMEM) for x in results])
    return loss.reshape(()), jnp.transpose(query_grad, (1, 0, 2)), page_grad


def solution(mesh):
    groups, members = mesh.shape["grp"], mesh.shape["dev"]
    split_spec = P(("grp", "dev"), None, None)
    return jax.shard_map(
        functools.partial(shards, groups, members),
        mesh=mesh,
        in_specs=(split_spec, split_spec, P()),
        out_specs=(P(), split_spec, split_spec),
        check_vma=False,
    )
```

```python
import functools
import math

import jax
import jax.numpy as jnp
from jax import lax
from jax.experimental import pallas as pl
from jax.experimental.pallas import tpu as pltpu
from jax.sharding import PartitionSpec as P

cap_value = 4.0
sharpness_divisor = 0.25
logit_scale = 8.0
z_weight = 0.001
highest = lax.Precision.HIGHEST
MESH = pl.DeviceIdType.MESH


def split(x):
    high = x.astype(jnp.bfloat16)
    low = (x - high.astype(jnp.float32)).astype(jnp.bfloat16)
    return high, low


def dot(a, b):
    return jnp.dot(a, b, preferred_element_type=jnp.float32)


def dot3(a, b):
    (a_high, a_low), (b_high, b_low) = a, b
    return dot(a_high, b_high) + (dot(a_high, b_low) + dot(a_low, b_high))


def kernel(
    groups, members, block, pad,
    query_hbm, page_hbm, positive_hbm,
    query_grad, page_grad,
    gathered, page, positive, rows, slopes_of, slopes_t, own_logits, logits, terms, arrived, weights,
    query_sem, page_sem, positive_sem, send_sems, recv_sems,
):
    count = groups * members
    group_blocks = members // block
    blocks = groups * group_blocks
    _, lines, spots, tokens, _ = gathered.shape
    lanes = own_logits.shape[-1]
    block_rows = block * pad
    group, member = lax.axis_index("grp"), lax.axis_index("dev")
    me = group * members + member
    line, spot = member // spots, lax.rem(member, spots)
    own_query = gathered.at[group, line, spot]
    own_line = gathered.at[group, :, spot]
    own_group = gathered.at[group]

    query_copy = pltpu.make_async_copy(query_hbm.at[:, 0], own_query, query_sem)
    page_copy = pltpu.make_async_copy(page_hbm.at[0], page, page_sem)
    positive_copy = pltpu.make_async_copy(positive_hbm, positive, positive_sem)
    query_copy.start()
    page_copy.start()
    positive_copy.start()

    def each(first, last, act):
        def step(k, carry):
            to_group = lax.rem(group + k // members, groups)
            to_member = lax.rem(member + k, members)
            act(to_group * members + to_member, (to_group, to_member))
            return carry

        lax.fori_loop(first, last, step, 0)

    def send(source, target, stage, device):
        pltpu.make_async_remote_copy(
            source, target, send_sems.at[stage], recv_sems.at[stage],
            device_id=device, device_id_type=MESH,
        ).start()

    def wait_for(whole, sem):
        pltpu.make_async_copy(whole, whole, sem).wait()

    def wait_all(buffer, size, sem):
        wait_for(buffer.at[pl.ds(0, size)], sem)

    def on_line(k):
        return group, lax.rem(line + k, lines) * spots + spot

    def on_spot(k):
        return group, line * spots + lax.rem(spot + k, spots)

    def on_group(k):
        return lax.rem(group + k, groups), member

    def partners(size, of, act):
        def step(k, carry):
            act(of(k))
            return carry

        lax.fori_loop(1, size, step, 0)

    first_part = gathered.at[0, pl.ds(0, lines - 1), 0]
    second_part = gathered.at[0, :, pl.ds(0, spots - 1)]
    third_part = gathered.at[pl.ds(0, groups - 1)]

    barrier = pltpu.get_barrier_semaphore()

    def greet(device):
        pl.semaphore_signal(barrier, inc=1, device_id=device, device_id_type=MESH)

    partners(lines, on_line, greet)
    partners(spots, on_spot, greet)
    partners(groups, on_group, greet)
    query_copy.wait()
    pl.semaphore_wait(barrier, lines + spots + groups - 3)
    partners(lines, on_line, lambda device: send(own_query, own_query, 0, device))

    page_copy.wait()
    positive_copy.wait()
    page_rows = page[...]
    page_columns = page_rows.T
    page_parts = split(page_rows)
    rows[...] = jnp.zeros_like(rows)

    def score(s, logit_row):
        b = lax.rem(group * group_blocks + s, blocks)
        first_line = lax.rem(b, group_blocks) * (block // spots)
        for q in range(block):
            rows[b, q * pad:q * pad + tokens, :] = gathered[
                b // group_blocks, first_line + q // spots, q % spots
            ]
        scores = jnp.dot(
            rows[b], page_columns, precision=highest, preferred_element_type=jnp.float32
        )
        tangent = jnp.tanh(scores / cap_value)
        grid = jnp.exp(tangent * (cap_value / sharpness_divisor))
        totals = jnp.sum(grid, axis=1, keepdims=True)
        peak = sharpness_divisor * jnp.log(totals)
        slopes_of[b] = grid * (1.0 - tangent * tangent) * ((logit_scale / tokens) / totals)
        row = lax.broadcasted_iota(jnp.int32, (block_rows, lanes), 0)
        lane = lax.broadcasted_iota(jnp.int32, (block_rows, lanes), 1)
        mine = (lane == b * block + row // pad) & (row % pad < tokens)
        return logit_row + jnp.sum(jnp.where(mine, peak, 0.0), axis=0, keepdims=True)

    def project(s, carry):
        b = lax.rem(group * group_blocks + s, blocks)
        slopes = slopes_of[b]
        term = dot3(split(slopes), page_parts)
        for q in range(block):
            terms[b * block + q] = term[q * pad:q * pad + tokens, :]
        slopes_t[b] = slopes.T
        return carry

    def send_term(peer, device):
        send(terms.at[peer], arrived.at[me], 4, device)

    wait_for(first_part, recv_sems.at[0])
    partners(spots, on_spot, lambda device: send(own_line, own_line, 1, device))
    wait_for(second_part, recv_sems.at[1])
    partners(groups, on_group, lambda device: send(own_group, own_group, 2, device))
    logit_row = jnp.zeros((1, lanes), jnp.float32)
    logit_row = lax.fori_loop(0, group_blocks, score, logit_row)
    lax.fori_loop(0, group_blocks, project, 0)
    wait_for(third_part, recv_sems.at[2])
    logit_row = lax.fori_loop(group_blocks, blocks, score, logit_row)
    own_logits[...] = logit_row * (logit_scale / tokens)
    logits[me] = own_logits[...]
    each(1, count, lambda peer, device: send(own_logits, logits.at[me], 3, device))
    each(1, members, send_term)
    lax.fori_loop(group_blocks, blocks, project, 0)
    each(members, count, send_term)

    wait_all(logits, count - 1, recv_sems.at[3])
    table = logits[:, 0, :][:, :count]
    of_page = lax.broadcasted_iota(jnp.int32, (count, count), 0)
    of_query = lax.broadcasted_iota(jnp.int32, (count, count), 1)
    chosen = (positive[...] == of_page).astype(jnp.float32)
    grid = jnp.exp(table)
    totals = jnp.sum(grid, axis=0, keepdims=True)
    log_totals = jnp.log(totals)
    matching = jnp.sum(chosen * table, axis=0, keepdims=True)
    losses = log_totals - matching + z_weight * log_totals * log_totals
    loss = jnp.sum(losses, axis=1, keepdims=True) / count
    query_grad[tokens] = jnp.broadcast_to(loss, query_grad.shape[1:])
    coefficients = ((1.0 + 2.0 * z_weight * log_totals) * grid / totals - chosen) / count
    of_me = jnp.sum(jnp.where(of_page == me, coefficients, 0.0), axis=0, keepdims=True)
    to_me = jnp.sum(jnp.where(of_query == me, coefficients, 0.0), axis=1, keepdims=True)
    weights[...] = jnp.broadcast_to(to_me, weights.shape)

    def gather_page(b, total):
        row = lax.broadcasted_iota(jnp.int32, (block_rows, count), 0)
        lane = lax.broadcasted_iota(jnp.int32, (block_rows, count), 1)
        mine = lane == b * block + row // pad
        factor = jnp.sum(jnp.where(mine, of_me, 0.0), axis=1, keepdims=True)
        return total + dot3(split(slopes_t[b]), split(rows[b] * factor))

    page_grad[...] = lax.fori_loop(0, blocks, gather_page, jnp.zeros(page_grad.shape, jnp.float32))

    wait_all(arrived, count - 1, recv_sems.at[4])
    arrived[me] = terms[me]

    def gather_query(p, total):
        return total + arrived[p] * weights[pl.ds(p, 1), :]

    total = lax.fori_loop(
        0, count, gather_query, jnp.zeros(arrived.shape[1:], jnp.float32), unroll=8
    )
    for i in range(tokens):
        query_grad[i] = total[i:i + 1, :]
    wait_for(first_part, send_sems.at[0])
    wait_for(second_part, send_sems.at[1])
    wait_for(third_part, send_sems.at[2])
    wait_all(logits, count - 1, send_sems.at[3])
    wait_all(terms, count - 1, send_sems.at[4])


def hand_over(query_grad, page_grad, loss_hbm, query_grad_hbm, page_grad_hbm, loss, sems):
    tokens = query_grad_hbm.shape[0]
    page_out = pltpu.make_async_copy(page_grad, page_grad_hbm.at[0], sems.at[0])
    query_out = pltpu.make_async_copy(
        query_grad.at[pl.ds(0, tokens)], query_grad_hbm, sems.at[1]
    )
    loss_out = pltpu.make_async_copy(loss, loss_hbm, sems.at[2])
    page_out.start()
    query_out.start()
    loss[...] = query_grad[tokens][:, :1]
    loss_out.start()
    page_out.wait()
    query_out.wait()
    loss_out.wait()


def shards(groups, members, queries, pages, positive):
    count = groups * members
    _, tokens, width = queries.shape
    page_tokens = pages.shape[1]
    block = math.gcd(members, 16)
    spots = math.gcd(members, 4)
    blocks = count // block
    pad = -(-tokens // 8) * 8
    lanes = max(128, -(-count // 128) * 128)
    anywhere = pl.BlockSpec(memory_space=pl.ANY)
    vmem = pl.BlockSpec(memory_space=pltpu.VMEM)
    float32 = jnp.float32
    results = pl.pallas_call(
        functools.partial(kernel, groups, members, block, pad),
        out_shape=(
            pltpu.VMEM((tokens + 1, 1, width), float32),
            pltpu.VMEM((page_tokens, width), float32),
        ),
        in_specs=[anywhere] * 3,
        out_specs=(vmem,) * 2,
        scratch_shapes=[
            pltpu.VMEM((groups, members // spots, spots, tokens, width), float32),
            pltpu.VMEM((page_tokens, width), float32),
            pltpu.VMEM((1, count), jnp.int32),
            pltpu.VMEM((blocks, block * pad, width), float32),
            pltpu.VMEM((blocks, block * pad, page_tokens), float32),
            pltpu.VMEM((blocks, page_tokens, block * pad), float32),
            pltpu.VMEM((1, lanes), float32),
            pltpu.VMEM((count, 1, lanes), float32),
            pltpu.VMEM((count, tokens, width), float32),
            pltpu.VMEM((count, tokens, width), float32),
            pltpu.VMEM((count, width), float32),
            pltpu.SemaphoreType.DMA,
            pltpu.SemaphoreType.DMA,
            pltpu.SemaphoreType.DMA,
            pltpu.SemaphoreType.DMA((5,)),
            pltpu.SemaphoreType.DMA((5,)),
        ],
        compiler_params=pltpu.CompilerParams(collective_id=0, has_side_effects=True),
    )(jnp.transpose(queries, (1, 0, 2)), pages, positive.reshape(1, count))
    loss, query_grad, page_grad = pl.pallas_call(
        hand_over,
        out_shape=(
            jax.ShapeDtypeStruct((1, 1), float32),
            jax.ShapeDtypeStruct((tokens, 1, width), float32),
            jax.ShapeDtypeStruct(pages.shape, float32),
        ),
        in_specs=[vmem] * 2,
        out_specs=(anywhere,) * 3,
        scratch_shapes=[pltpu.VMEM((1, 1), float32), pltpu.SemaphoreType.DMA((3,))],
        compiler_params=pltpu.CompilerParams(vmem_limit_bytes=1 << 20),
    )(*[pltpu.with_memory_space_constraint(x, pltpu.VMEM) for x in results])
    return loss.reshape(()), jnp.transpose(query_grad, (1, 0, 2)), page_grad


def solution(mesh):
    groups, members = mesh.shape["grp"], mesh.shape["dev"]
    split_spec = P(("grp", "dev"), None, None)
    return jax.shard_map(
        functools.partial(shards, groups, members),
        mesh=mesh,
        in_specs=(split_spec, split_spec, P()),
        out_specs=(P(), split_spec, split_spec),
        check_vma=False,
    )
```

```python
import functools
import math

import jax
import jax.numpy as jnp
from jax import lax
from jax.experimental import pallas as pl
from jax.experimental.pallas import tpu as pltpu
from jax.sharding import PartitionSpec as P

cap_value = 4.0
sharpness_divisor = 0.25
logit_scale = 8.0
z_weight = 0.001
highest = lax.Precision.HIGHEST
MESH = pl.DeviceIdType.MESH


def split(x):
    high = x.astype(jnp.bfloat16)
    low = (x - high.astype(jnp.float32)).astype(jnp.bfloat16)
    return high, low


def dot(a, b):
    return jnp.dot(a, b, preferred_element_type=jnp.float32)


def dot3(a, b):
    (a_high, a_low), (b_high, b_low) = a, b
    return dot(a_high, b_high) + (dot(a_high, b_low) + dot(a_low, b_high))


def kernel(
    groups, members, block, pad,
    query_hbm, page_hbm, positive_hbm,
    query_grad, page_grad,
    gathered, page, positive, rows, slopes_of, slopes_t, own_logits, logits, terms, arrived, weights,
    query_sem, page_sem, positive_sem, send_sems, recv_sems,
):
    count = groups * members
    group_blocks = members // block
    blocks = groups * group_blocks
    tokens = gathered.shape[1]
    lanes = own_logits.shape[-1]
    block_rows = block * pad
    group, member = lax.axis_index("grp"), lax.axis_index("dev")
    me = group * members + member

    query_copy = pltpu.make_async_copy(query_hbm.at[:, 0], gathered.at[me], query_sem)
    page_copy = pltpu.make_async_copy(page_hbm.at[0], page, page_sem)
    positive_copy = pltpu.make_async_copy(positive_hbm, positive, positive_sem)
    query_copy.start()
    page_copy.start()
    positive_copy.start()

    def each(first, last, act):
        def step(k, carry):
            to_group = lax.rem(group + k // members, groups)
            to_member = lax.rem(member + k, members)
            act(to_group * members + to_member, (to_group, to_member))
            return carry

        lax.fori_loop(first, last, step, 0)

    def send(source, target, stage, device):
        pltpu.make_async_remote_copy(
            source, target, send_sems.at[stage], recv_sems.at[stage],
            device_id=device, device_id_type=MESH,
        ).start()

    def wait_all(buffer, size, sem):
        whole = buffer.at[pl.ds(0, size)]
        pltpu.make_async_copy(whole, whole, sem).wait()

    barrier = pltpu.get_barrier_semaphore()
    each(1, members, lambda peer, device: pl.semaphore_signal(
        barrier, inc=1, device_id=device, device_id_type=MESH))

    def greet_group(k, carry):
        pl.semaphore_signal(
            barrier, inc=1, device_id=(lax.rem(group + k, groups), member), device_id_type=MESH
        )
        return carry

    lax.fori_loop(1, groups, greet_group, 0)
    query_copy.wait()
    pl.semaphore_wait(barrier, members + groups - 2)
    each(1, members, lambda peer, device: send(gathered.at[me], gathered.at[me], 0, device))

    page_copy.wait()
    positive_copy.wait()
    page_rows = page[...]
    page_columns = page_rows.T
    page_parts = split(page_rows)
    rows[...] = jnp.zeros_like(rows)

    def score(s, logit_row):
        b = lax.rem(group * group_blocks + s, blocks)
        for q in range(block):
            rows[b, q * pad:q * pad + tokens, :] = gathered[b * block + q]
        scores = jnp.dot(
            rows[b], page_columns, precision=highest, preferred_element_type=jnp.float32
        )
        tangent = jnp.tanh(scores / cap_value)
        grid = jnp.exp(tangent * (cap_value / sharpness_divisor))
        totals = jnp.sum(grid, axis=1, keepdims=True)
        peak = sharpness_divisor * jnp.log(totals)
        slopes_of[b] = grid * (1.0 - tangent * tangent) * ((logit_scale / tokens) / totals)
        row = lax.broadcasted_iota(jnp.int32, (block_rows, lanes), 0)
        lane = lax.broadcasted_iota(jnp.int32, (block_rows, lanes), 1)
        mine = (lane == b * block + row // pad) & (row % pad < tokens)
        return logit_row + jnp.sum(jnp.where(mine, peak, 0.0), axis=0, keepdims=True)

    def project(s, carry):
        b = lax.rem(group * group_blocks + s, blocks)
        slopes = slopes_of[b]
        term = dot3(split(slopes), page_parts)
        for q in range(block):
            terms[b * block + q] = term[q * pad:q * pad + tokens, :]
        slopes_t[b] = slopes.T
        return carry

    def send_term(peer, device):
        send(terms.at[peer], arrived.at[me], 3, device)

    wait_all(gathered, members - 1, recv_sems.at[0])
    own_group = gathered.at[pl.ds(group * members, members)]

    def pass_on(k, carry):
        send(own_group, own_group, 1, (lax.rem(group + k, groups), member))
        return carry

    lax.fori_loop(1, groups, pass_on, 0)
    logit_row = jnp.zeros((1, lanes), jnp.float32)
    logit_row = lax.fori_loop(0, group_blocks, score, logit_row)
    lax.fori_loop(0, group_blocks, project, 0)
    each(1, members, send_term)
    wait_all(gathered, count - members, recv_sems.at[1])
    logit_row = lax.fori_loop(group_blocks, blocks, score, logit_row)
    own_logits[...] = logit_row * (logit_scale / tokens)
    logits[me] = own_logits[...]
    each(1, count, lambda peer, device: send(own_logits, logits.at[me], 2, device))
    lax.fori_loop(group_blocks, blocks, project, 0)
    each(members, count, send_term)

    wait_all(logits, count - 1, recv_sems.at[2])
    table = logits[:, 0, :][:, :count]
    of_page = lax.broadcasted_iota(jnp.int32, (count, count), 0)
    of_query = lax.broadcasted_iota(jnp.int32, (count, count), 1)
    chosen = (positive[...] == of_page).astype(jnp.float32)
    grid = jnp.exp(table)
    totals = jnp.sum(grid, axis=0, keepdims=True)
    log_totals = jnp.log(totals)
    matching = jnp.sum(chosen * table, axis=0, keepdims=True)
    losses = log_totals - matching + z_weight * log_totals * log_totals
    loss = jnp.sum(losses, axis=1, keepdims=True) / count
    query_grad[tokens] = jnp.broadcast_to(loss, query_grad.shape[1:])
    coefficients = ((1.0 + 2.0 * z_weight * log_totals) * grid / totals - chosen) / count
    of_me = jnp.sum(jnp.where(of_page == me, coefficients, 0.0), axis=0, keepdims=True)
    to_me = jnp.sum(jnp.where(of_query == me, coefficients, 0.0), axis=1, keepdims=True)
    weights[...] = jnp.broadcast_to(to_me, weights.shape)

    def gather_page(b, total):
        row = lax.broadcasted_iota(jnp.int32, (block_rows, count), 0)
        lane = lax.broadcasted_iota(jnp.int32, (block_rows, count), 1)
        mine = lane == b * block + row // pad
        factor = jnp.sum(jnp.where(mine, of_me, 0.0), axis=1, keepdims=True)
        return total + dot3(split(slopes_t[b]), split(rows[b] * factor))

    page_grad[...] = lax.fori_loop(0, blocks, gather_page, jnp.zeros(page_grad.shape, jnp.float32))

    wait_all(arrived, count - 1, recv_sems.at[3])
    arrived[me] = terms[me]

    def gather_query(p, total):
        return total + arrived[p] * weights[pl.ds(p, 1), :]

    total = lax.fori_loop(
        0, count, gather_query, jnp.zeros(arrived.shape[1:], jnp.float32), unroll=8
    )
    for i in range(tokens):
        query_grad[i] = total[i:i + 1, :]
    wait_all(gathered, members - 1, send_sems.at[0])
    wait_all(gathered, count - members, send_sems.at[1])
    wait_all(logits, count - 1, send_sems.at[2])
    wait_all(terms, count - 1, send_sems.at[3])


def hand_over(query_grad, page_grad, loss_hbm, query_grad_hbm, page_grad_hbm, loss, sems):
    tokens = query_grad_hbm.shape[0]
    page_out = pltpu.make_async_copy(page_grad, page_grad_hbm.at[0], sems.at[0])
    query_out = pltpu.make_async_copy(
        query_grad.at[pl.ds(0, tokens)], query_grad_hbm, sems.at[1]
    )
    loss_out = pltpu.make_async_copy(loss, loss_hbm, sems.at[2])
    page_out.start()
    query_out.start()
    loss[...] = query_grad[tokens][:, :1]
    loss_out.start()
    page_out.wait()
    query_out.wait()
    loss_out.wait()


def shards(groups, members, queries, pages, positive):
    count = groups * members
    _, tokens, width = queries.shape
    page_tokens = pages.shape[1]
    block = math.gcd(members, 16)
    blocks = count // block
    pad = -(-tokens // 8) * 8
    lanes = max(128, -(-count // 128) * 128)
    anywhere = pl.BlockSpec(memory_space=pl.ANY)
    vmem = pl.BlockSpec(memory_space=pltpu.VMEM)
    float32 = jnp.float32
    results = pl.pallas_call(
        functools.partial(kernel, groups, members, block, pad),
        out_shape=(
            pltpu.VMEM((tokens + 1, 1, width), float32),
            pltpu.VMEM((page_tokens, width), float32),
        ),
        in_specs=[anywhere] * 3,
        out_specs=(vmem,) * 2,
        scratch_shapes=[
            pltpu.VMEM((count, tokens, width), float32),
            pltpu.VMEM((page_tokens, width), float32),
            pltpu.VMEM((1, count), jnp.int32),
            pltpu.VMEM((blocks, block * pad, width), float32),
            pltpu.VMEM((blocks, block * pad, page_tokens), float32),
            pltpu.VMEM((blocks, page_tokens, block * pad), float32),
            pltpu.VMEM((1, lanes), float32),
            pltpu.VMEM((count, 1, lanes), float32),
            pltpu.VMEM((count, tokens, width), float32),
            pltpu.VMEM((count, tokens, width), float32),
            pltpu.VMEM((count, width), float32),
            pltpu.SemaphoreType.DMA,
            pltpu.SemaphoreType.DMA,
            pltpu.SemaphoreType.DMA,
            pltpu.SemaphoreType.DMA((4,)),
            pltpu.SemaphoreType.DMA((4,)),
        ],
        compiler_params=pltpu.CompilerParams(collective_id=0, has_side_effects=True),
    )(jnp.transpose(queries, (1, 0, 2)), pages, positive.reshape(1, count))
    loss, query_grad, page_grad = pl.pallas_call(
        hand_over,
        out_shape=(
            jax.ShapeDtypeStruct((1, 1), float32),
            jax.ShapeDtypeStruct((tokens, 1, width), float32),
            jax.ShapeDtypeStruct(pages.shape, float32),
        ),
        in_specs=[vmem] * 2,
        out_specs=(anywhere,) * 3,
        scratch_shapes=[pltpu.VMEM((1, 1), float32), pltpu.SemaphoreType.DMA((3,))],
        compiler_params=pltpu.CompilerParams(vmem_limit_bytes=1 << 20),
    )(*[pltpu.with_memory_space_constraint(x, pltpu.VMEM) for x in results])
    return loss.reshape(()), jnp.transpose(query_grad, (1, 0, 2)), page_grad


def solution(mesh):
    groups, members = mesh.shape["grp"], mesh.shape["dev"]
    split_spec = P(("grp", "dev"), None, None)
    return jax.shard_map(
        functools.partial(shards, groups, members),
        mesh=mesh,
        in_specs=(split_spec, split_spec, P()),
        out_specs=(P(), split_spec, split_spec),
        check_vma=False,
    )
```
